32 devices in a mesh: chars: 2 (over x), prow: 16 (over z, y, core).
Axes of the slice: x: 2, y: 2, z: 4, core: 2. Of those that a mesh axis runs over, the one named last changes fastest.
Arguments:
- queries: bfloat16 [8192, 512], P(('chars', 'prow')), parts along dimension 0, may hold values from -8 to 8
- keys: bfloat16 [8192, 512], P(('chars', 'prow')), parts along dimension 0, may hold values from -8 to 8
- values: bfloat16 [8192, 512], P(('chars', 'prow')), parts along dimension 0, may hold values from -6 to 6
- out_grad: bfloat16 [8192, 512], P(('chars', 'prow')), parts along dimension 0, may hold values from -6 to 6
- valid_counts: int32 [32, 4], P('chars'), parts along dimension 0, may hold values from 1 to 64
- landmark_cols: int32 [32], P('chars'), parts along dimension 0, may hold values from 0 to 3
- landmark_rows: int32 [32, 4], P(('chars', 'prow')), parts along dimension 0, may hold values from 0 to 15, as said below
Outputs:
- attn_out: bfloat16 [8192, 512], P(('chars', 'prow')), parts along dimension 0
- query_grad: bfloat16 [8192, 512], P(('chars', 'prow')), parts along dimension 0
- key_grad: bfloat16 [8192, 512], P(('chars', 'prow')), parts along dimension 0
- value_grad: bfloat16 [8192, 512], P(('chars', 'prow')), parts along dimension 0
The draws below stay inside these ranges and needn't reach their ends.
There are 2 independent parts, one for each index of `chars`. The reference program is written for one: setup_inputs(seed, part) draws one part's arguments, and reference() takes and returns one part's arrays. A program takes and returns all parts, laid end to end along the dimension named above; each array names one. Nothing has to cross between parts.
Inputs may be any that keep to these rules, and one draw needn't show every extreme that they name: `landmark_rows`: the 4 entries of each row are distinct.
All inputs are finite; a program needn't handle non-finite values.
Results may differ from the reference program's by a relative error of at most 0.012.
The reference program's roundings to bfloat16 on the way count: a program that leaves them out, or rounds other values in their place, can miss the bound.
Values may be sent and summed in bfloat16 or wider, within the bound.
A program may use at most 192 MiB of HBM per device.

```python
import math
import jax
import jax.numpy as jnp
from jax import lax

HEADS = 8
HD = 64
WIDTH = 512
BLK = 64
NLAND = 4
PC = 4
NROWS = 16
TOKENS = 4096


def drawn_field(key, member):
    base_key = jax.random.fold_in(key, 7 + member)
    drawn = jnp.clip(jax.random.normal(jax.random.fold_in(base_key, 2), (TOKENS, WIDTH)), -6.0, 6.0)
    return drawn.astype(jnp.bfloat16)


def draw_queries(key, part):
    return drawn_field(key, 0)


def draw_keys(key, part):
    return drawn_field(key, 1)


def draw_landmark_rows(key, part):
    row_keys = jax.vmap(lambda index: jax.random.fold_in(key, index))(jnp.arange(NROWS))
    orders = jax.vmap(lambda row_key: jax.random.permutation(row_key, NROWS))(row_keys)
    return orders[:, :NLAND].astype(jnp.int32)


def place_ends(values, rng, least, high):
    dims = values.shape
    place = [jax.random.randint(jax.random.fold_in(rng, axis), (), 0, dims[axis]) for axis in range(len(dims))]
    values = values.at[tuple(place)].set(least)
    longest = dims.index(max(dims))
    place[longest] = (place[longest] + 1) % dims[longest]
    return values.at[tuple(place)].set(high)


def block_scale(key, dims, cuts, least, largest):
    level = 1.0
    for axis_at, parts in cuts:
        heights = jax.random.uniform(jax.random.fold_in(jax.random.fold_in(key, 6), axis_at), (parts,), jnp.float32, least / len(cuts), largest / len(cuts))
        level = level * jnp.repeat(jnp.exp(heights), dims[axis_at] // parts).reshape((-1,) + (1,) * (len(dims) - 1 - axis_at))
    return level


def normal_values(key, extent, deviation, bound, shards=(), kind=jnp.bfloat16):
    entries = deviation * jax.random.normal(key, extent, jnp.float32)
    if shards:
        entries = entries * block_scale(key, extent, shards, -0.22, 0.18)
    return jnp.clip(entries, -bound, bound).astype(kind)


def setup_inputs(seed: int = 0, part: int = 0) -> dict:
    arg_keys = jax.random.split(jax.random.key(seed), 8)
    own_keys = jax.random.split(jax.random.fold_in(arg_keys[7], part), 8)
    queries = draw_queries(jax.random.fold_in(jax.random.fold_in(arg_keys[7], part), 71), part)
    keys = draw_keys(jax.random.fold_in(jax.random.fold_in(arg_keys[7], part), 71), part)
    values = normal_values(own_keys[2], (TOKENS, WIDTH), 1.0, 6.0, ((0, 16),))
    out_grad = normal_values(own_keys[3], (TOKENS, WIDTH), 1.0, 6.0, ((0, 16),))
    valid_counts = place_ends(jax.random.randint(own_keys[4], (NROWS, PC), 1, BLK + 1), jax.random.fold_in(own_keys[4], 1), 1, BLK).astype(jnp.int32)
    landmark_cols = place_ends(jax.random.randint(own_keys[5], (NROWS,), 0, PC), jax.random.fold_in(own_keys[5], 1), 0, PC - 1).astype(jnp.int32)
    landmark_rows = draw_landmark_rows(jax.random.fold_in(jax.random.fold_in(arg_keys[7], part), 71), part)
    return dict(queries=queries, keys=keys, values=values, out_grad=out_grad, valid_counts=valid_counts, landmark_cols=landmark_cols, landmark_rows=landmark_rows)


masked_score = -1e+30

def product(form, left, right):
    return jnp.einsum(form, left.astype(jnp.float32), right.astype(jnp.float32), precision=lax.Precision.HIGHEST)

def window_stack(near_rows, columns):
    pieces = [near_rows[row_off, col_off:col_off + columns] for row_off in range(3) for col_off in range(3)]
    stacked = jnp.stack(pieces, axis=1)
    return stacked.reshape(columns, 9 * stacked.shape[2], stacked.shape[3])

def window_mask(count_near, columns, block_len):
    pieces = [count_near[row_off, col_off:col_off + columns] for row_off in range(3) for col_off in range(3)]
    counts = jnp.stack(pieces, axis=1)
    position = jnp.arange(block_len)
    return (position[None, None, :] < counts[:, :, None]).reshape(columns, 9 * block_len)

def spread(grad_window, columns, block_len):
    pieces = grad_window.reshape(columns, 9, block_len, grad_window.shape[-1])
    layers = []
    for row_off in range(3):
        left = jnp.pad(pieces[:, row_off * 3], ((0, 2), (0, 0), (0, 0)))
        middle = jnp.pad(pieces[:, row_off * 3 + 1], ((1, 1), (0, 0), (0, 0)))
        right = jnp.pad(pieces[:, row_off * 3 + 2], ((2, 0), (0, 0), (0, 0)))
        layers.append(left + middle + right)
    return jnp.stack(layers)

def attend(query_blocks, grad_raw, keys_win, values_win, mask_win, keys_land, values_land, mask_land, query_valid):
    score_scale = 1.0 / math.sqrt(query_blocks.shape[-1])
    scores_win = product('cqhe,cwhe->chqw', query_blocks, keys_win) * score_scale
    scores_land = product('cqhe,lhe->chql', query_blocks, keys_land) * score_scale
    scores_win = jnp.where(mask_win[:, None, None, :], scores_win, masked_score)
    scores_land = jnp.where(mask_land[None, None, None, :], scores_land, masked_score)
    row_max = jnp.maximum(lax.optimization_barrier(jnp.max(scores_win, axis=-1)), lax.optimization_barrier(jnp.max(scores_land, axis=-1)))
    exp_total = lax.optimization_barrier(jnp.sum(jnp.exp(scores_win - row_max[..., None]), axis=-1)) + lax.optimization_barrier(jnp.sum(jnp.exp(scores_land - row_max[..., None]), axis=-1))
    log_total = row_max + jnp.log(exp_total)
    probs_win = jnp.exp(scores_win - log_total[..., None])
    probs_land = jnp.exp(scores_land - log_total[..., None])
    low_win = probs_win.astype(jnp.bfloat16)
    low_land = probs_land.astype(jnp.bfloat16)
    mixed_out = product('chqw,cwhe->cqhe', low_win, values_win) + product('chql,lhe->cqhe', low_land, values_land)
    query_mask = query_valid[:, :, None, None]
    attn_part = jnp.where(query_mask, mixed_out, 0.0).astype(jnp.bfloat16)
    grad_in = jnp.where(query_mask, grad_raw, jnp.zeros_like(grad_raw))
    row_delta = lax.optimization_barrier(jnp.sum(grad_in.astype(jnp.float32) * mixed_out, axis=-1))
    row_delta = jnp.transpose(row_delta, (0, 2, 1))[..., None]
    dprob_win = product('cqhe,cwhe->chqw', grad_in, values_win)
    dprob_land = product('cqhe,lhe->chql', grad_in, values_land)
    dscore_win = (probs_win * (dprob_win - row_delta) * score_scale).astype(jnp.bfloat16)
    dscore_land = (probs_land * (dprob_land - row_delta) * score_scale).astype(jnp.bfloat16)
    query_part = (product('chqw,cwhe->cqhe', dscore_win, keys_win) + product('chql,lhe->cqhe', dscore_land, keys_land)).astype(jnp.bfloat16)
    kgrad_win = product('chqw,cqhe->cwhe', dscore_win, query_blocks)
    vgrad_win = product('chqw,cqhe->cwhe', low_win, grad_in)
    kgrad_land = product('chql,cqhe->lhe', dscore_land, query_blocks)
    vgrad_land = product('chql,cqhe->lhe', low_land, grad_in)
    return (attn_part, query_part, kgrad_win, vgrad_win, kgrad_land, vgrad_land)

def reference(queries, keys, values, out_grad, valid_counts, landmark_cols, landmark_rows):
    model_width = HEADS * HD
    key_value = jnp.concatenate([keys, values], axis=1).reshape(NROWS, PC, BLK, 2 * model_width)
    kv_padded = jnp.pad(key_value, ((1, 1), (1, 1), (0, 0), (0, 0)))
    count_padded = jnp.pad(valid_counts, ((1, 1), (1, 1)))
    row_ids = jnp.arange(NROWS, dtype=jnp.int32)
    land_panel = key_value[row_ids, landmark_cols]
    panel_counts = valid_counts[row_ids, landmark_cols]
    query_rows = queries.reshape(NROWS, PC, BLK, HEADS, HD)
    grad_rows = out_grad.reshape(NROWS, PC, BLK, HEADS, HD)
    position = jnp.arange(BLK)

    def row_step(state_pair, row_index):
        window_grads, land_grads = state_pair
        near_rows = lax.dynamic_slice_in_dim(kv_padded, row_index, 3, 0)
        count_near = lax.dynamic_slice_in_dim(count_padded, row_index, 3, 0)
        chosen_rows = landmark_rows[row_index]
        chosen = land_panel[chosen_rows]
        chosen_counts = panel_counts[chosen_rows]
        stacked = window_stack(near_rows, PC)
        keys_win = stacked[..., :model_width].reshape(PC, 9 * BLK, HEADS, HD)
        values_win = stacked[..., model_width:].reshape(PC, 9 * BLK, HEADS, HD)
        mask_win = window_mask(count_near, PC, BLK)
        keys_land = chosen[..., :model_width].reshape(NLAND * BLK, HEADS, HD)
        values_land = chosen[..., model_width:].reshape(NLAND * BLK, HEADS, HD)
        mask_land = (position[None, :] < chosen_counts[:, None]).reshape(NLAND * BLK)
        query_valid = position[None, :] < valid_counts[row_index][:, None]
        attn_part, query_part, kgrad_win, vgrad_win, kgrad_land, vgrad_land = attend(query_rows[row_index], grad_rows[row_index], keys_win, values_win, mask_win, keys_land, values_land, mask_land, query_valid)
        grad_window = jnp.concatenate([kgrad_win.reshape(PC, 9 * BLK, model_width), vgrad_win.reshape(PC, 9 * BLK, model_width)], axis=-1)
        summed = spread(grad_window, PC, BLK)
        current = lax.dynamic_slice_in_dim(window_grads, row_index, 3, 0)
        window_grads = lax.dynamic_update_slice_in_dim(window_grads, current + summed, row_index, 0)
        grad_land = jnp.concatenate([kgrad_land.reshape(NLAND, BLK, model_width), vgrad_land.reshape(NLAND, BLK, model_width)], axis=-1)
        land_grads = land_grads.at[chosen_rows].add(grad_land)
        return ((window_grads, land_grads), (attn_part, query_part))
    start_state = (jnp.zeros((NROWS + 2, PC + 2, BLK, 2 * model_width), jnp.float32), jnp.zeros((NROWS, BLK, 2 * model_width), jnp.float32))
    final_state, row_outputs = lax.scan(row_step, start_state, row_ids)
    window_grads, land_grads = final_state
    attn_rows, qgrad_rows = row_outputs
    all_grads = window_grads[1:-1, 1:-1].at[row_ids, landmark_cols].add(land_grads)
    attn_out = attn_rows.reshape(TOKENS, model_width)
    query_grad = qgrad_rows.reshape(TOKENS, model_width)
    key_grad = all_grads[..., :model_width].astype(jnp.bfloat16).reshape(TOKENS, model_width)
    value_grad = all_grads[..., model_width:].astype(jnp.bfloat16).reshape(TOKENS, model_width)
    return (attn_out, query_grad, key_grad, value_grad)
```

```python
import functools

import jax
import jax.numpy as jnp
from jax import lax
from jax.experimental import pallas as pl
from jax.experimental.pallas import tpu as pltpu
from jax.sharding import PartitionSpec as P

HEADS = 8
HD = 64
BLK = 64
NLAND = 4
PC = 4
WIDTH = HEADS * HD
ROWS = PC * BLK
KEYS = 3 * ROWS + NLAND * BLK
F32 = jnp.float32
BF16 = jnp.bfloat16
MESH = pl.DeviceIdType.MESH
masked_score = -1e30
WIN = 3 * ROWS
VMEM_LIMIT = 60 * 1024 * 1024


def dot(a, b):
    return lax.dot_general(a, b, (((1,), (0,)), ((), ())), preferred_element_type=F32)


def remote(src, dst, send, recv, device):
    return pltpu.make_async_remote_copy(
        src_ref=src,
        dst_ref=dst,
        send_sem=send,
        recv_sem=recv,
        device_id={"prow": device},
        device_id_type=MESH,
    )


def position():
    me = lax.axis_index("prow")
    return me, me // 4, me % 4


def neighbours(n):
    me, z, p = position()
    last = n // 4 - 1
    found = [(4 * z + i, p != i) for i in range(4)]
    for step in (1, 2):
        found.append((me + 4 * step, z + step <= last))
        found.append((me - 4 * step, z - step >= 0))
    return found


def greet(n):
    barrier = pltpu.get_barrier_semaphore()
    for device, exists in neighbours(n):

        @pl.when(exists)
        def _():
            pl.semaphore_signal(barrier, inc=1, device_id={"prow": device}, device_id_type=MESH)


def met(n):
    count = 0
    for _, exists in neighbours(n):
        count = count + jnp.where(exists, 1, 0)
    pl.semaphore_wait(pltpu.get_barrier_semaphore(), count)


def fused_kernel(
    n,
    cols_ref,
    rows_ref,
    counts_ref,
    q_ref,
    k_ref,
    v_ref,
    do_ref,
    attn_ref,
    qgrad_ref,
    kgrad_ref,
    vgrad_ref,
    rows_tx,
    rows_rx,
    rows_quad,
    land_tx,
    kv_tx,
    qd_tx,
    panel,
    kv,
    kv_t,
    qd,
    qd_t,
    lkv,
    lkv_t,
    bias,
    e_win,
    top_win,
    sum_win,
    low_win,
    ds_win,
    grads,
    g_land,
    o_tx,
    o_rx,
    edge_tx,
    edge_rx,
    g_tx,
    g_rx,
    part,
    part_tx,
    relay_rx,
    owner_rx,
    total,
    total_tx,
    total_rx,
    local_sem,
    rows_s,
    rows_r,
    land_s,
    land_r,
    kv_s,
    kv_r,
    qd_s,
    qd_r,
    panel_up,
    panel_dn,
    panel_far,
    panel_r,
    halo_s,
    halo_r,
    o_s,
    o_r,
    edge_s,
    edge_r,
    g_s,
    g_r,
    relay_s,
    relay_r,
    owner_s,
    owner_r,
    total_s,
    total_r,
):
    me, z, p = position()
    depth = n // 4
    last = depth - 1
    quad = range(4)
    own_col = cols_ref[me]
    greet(n)

    def span(i):
        return slice(i * ROWS, (i + 1) * ROWS)

    def dyn_span(i):
        return pl.ds(pl.multiple_of(i * ROWS, ROWS), ROWS)

    def cols(i):
        return slice(i * 128, (i + 1) * 128)

    k_own = k_ref[own_col]
    v_own = v_ref[own_col]
    lane = lax.broadcasted_iota(jnp.int32, (8, 128), 1)
    ints = jnp.zeros((8, 128), jnp.int32)
    for j in range(NLAND):
        ints = jnp.where(lane == j, rows_ref[0, j], ints)
    rows_tx[...] = ints
    rows_rx[p] = ints
    k_rows = k_ref[...].reshape(ROWS, WIDTH)
    v_rows = v_ref[...].reshape(ROWS, WIDTH)
    for i in quad:
        land_tx[i, :, :128] = k_own[:, cols(i)]
        land_tx[i, :, 128:] = v_own[:, cols(i)]
        kv_tx[i, :, :128] = k_rows[:, cols(i)]
        kv_tx[i, :, 128:] = v_rows[:, cols(i)]

    @pl.when(z == 0)
    def _():
        kv[span(0)] = jnp.zeros((ROWS, 256), BF16)

    @pl.when(z == last)
    def _():
        kv[span(5)] = jnp.zeros((ROWS, 256), BF16)

    met(n)

    def rows_to(i):
        return remote(rows_tx, rows_rx.at[p], rows_s.at[i], rows_r.at[p], 4 * z + i)

    def rows_from(i):
        return remote(rows_tx, rows_rx.at[i], rows_s.at[i], rows_r.at[i], 4 * z + i)

    def land_to(i):
        return remote(land_tx.at[i], panel.at[me], land_s.at[i], land_r.at[p], 4 * z + i)

    def land_from(i):
        return remote(land_tx.at[i], panel.at[4 * z + i], land_s.at[i], land_r.at[i], 4 * z + i)

    def kv_to(i):
        return remote(kv_tx.at[i], kv.at[dyn_span(1 + p)], kv_s.at[i], kv_r.at[p], 4 * z + i)

    def kv_from(i):
        return remote(kv_tx.at[i], kv.at[span(1 + i)], kv_s.at[i], kv_r.at[i], 4 * z + i)

    def qd_to(i):
        return remote(qd_tx.at[i], qd.at[dyn_span(p)], qd_s.at[i], qd_r.at[p], 4 * z + i)

    def qd_from(i):
        return remote(qd_tx.at[i], qd.at[span(i)], qd_s.at[i], qd_r.at[i], 4 * z + i)

    def others(act):
        for i in quad:
            pl.when(p != i)(lambda: act(i))

    def panel_to(zz, step):
        place = panel.at[pl.ds(4 * zz, 4)]
        if step == 1:
            send = panel_up.at[zz]
        elif step == -1:
            send = panel_dn.at[zz]
        else:
            send = panel_far.at[0 if step > 0 else 1]
        return remote(place, place, send, panel_r.at[zz], me + 4 * step)

    def panel_own(act):
        for step in (1, -1, 2, -2):
            exists = z + step <= last if step > 0 else z + step >= 0
            pl.when(exists)(lambda: act(panel_to(z, step)))

    def each_side(s, act):
        pl.when(z - s >= 0)(lambda: act(z - s, 1, z < last))
        pl.when(z + s <= last)(lambda: act(z + s, -1, z > 0))

    def panel_relay(s):
        def step(zz, way, more):
            panel_to(zz, way).wait_recv()
            pl.when(more)(lambda: panel_to(zz, way).start())

        each_side(s, step)

    def panel_near():
        each_side(1, lambda zz, way, more: panel_to(zz, way).wait_recv())

    def halo_up():
        return remote(kv.at[span(4)], kv.at[span(0)], halo_s.at[0], halo_r.at[0], me + 4)

    def halo_dn():
        return remote(kv.at[span(1)], kv.at[span(5)], halo_s.at[1], halo_r.at[1], me - 4)

    pos = lax.broadcasted_iota(jnp.int32, (BLK, ROWS), 0)
    qcol = lax.broadcasted_iota(jnp.int32, (BLK, ROWS), 1) // BLK

    def window_bias(i):
        for a in range(3):
            row = 4 * z + i + a - 1
            inside = jnp.logical_and(row >= 0, row < n)
            safe = jnp.clip(row, 0, n - 1)
            for b in range(PC):
                count = jnp.where(inside, counts_ref[b, safe], 0)
                ok = (pos < count) & (qcol >= b - 1) & (qcol <= b + 1)
                base = a * ROWS + b * BLK
                bias[i, base : base + BLK] = jnp.where(ok, 0.0, masked_score)

    def set_queries():
        tpos = lax.broadcasted_iota(jnp.int32, (BLK, WIDTH), 0)
        for b in range(PC):
            at = slice(b * BLK, (b + 1) * BLK)
            part_q = q_ref[at] * 0.125
            part_d = do_ref[at].astype(F32)
            part_d = jnp.where(tpos < counts_ref[b, me], part_d, 0.0).astype(BF16)
            for i in quad:
                qd_tx[i, at, :128] = part_q[:, cols(i)]
                qd_tx[i, at, 128:] = part_d[:, cols(i)]

    def turn(a):
        kv_t[:, span(a)] = kv[span(a)].T

    def turn_queries(i):
        qd_t[:, span(i)] = qd[span(i)].T

    def take_rows():
        others(lambda i: rows_from(i).wait_recv())
        copy = pltpu.make_async_copy(rows_rx, rows_quad, local_sem.at[0])
        copy.start()
        copy.wait()

    def take_landmarks(i):
        for j in range(NLAND):
            row = rows_quad[i, 0, j]
            count = counts_ref[cols_ref[row], row]
            base = WIN + j * BLK
            bias[i, base : base + BLK] = jnp.where(pos < count, 0.0, masked_score)
            block = panel[row]
            at = slice(j * BLK, (j + 1) * BLK)
            lkv[i, at] = block
            lkv_t[i, :, at] = block.T

    zero = jnp.zeros((HD, ROWS), BF16)

    def padded(rows_t, h):
        return jnp.concatenate([rows_t, zero] if h == 0 else [zero, rows_t], axis=0)

    def window_scores(i):
        k2 = kv[i * ROWS : i * ROWS + WIN, 0:128]
        for h in range(2):
            head = 2 * i + h
            s = dot(k2, padded(qd_t[h * HD : (h + 1) * HD, span(i)], h)) + bias[i, 0:WIN]
            top = jnp.max(s, axis=0, keepdims=True)
            e = jnp.exp(s - top)
            e_win[head] = e
            top_win[head] = top
            sum_win[head] = jnp.sum(e, axis=0, keepdims=True)

    left = lax.broadcasted_iota(jnp.int32, (ROWS, 128), 1) < HD

    def halved(block, h):
        keep = left if h == 0 else jnp.logical_not(left)
        return jnp.where(keep, block.astype(F32), 0.0).astype(BF16)

    lanes = lax.broadcasted_iota(jnp.int32, (1, ROWS), 1)

    def landmarks(i):
        win = slice(i * ROWS, i * ROWS + WIN)
        k2 = lkv[i, :, 0:128]
        v2 = lkv[i, :, 128:256]
        v2w = kv[win, 128:256]
        q2 = qd[span(i), 0:128]
        do2 = qd[span(i), 128:256]
        dk2 = 0.0
        dv2 = 0.0
        mixes = []
        dqs = []
        for h in range(2):
            head = 2 * i + h
            krows = slice(h * HD, (h + 1) * HD)
            vrows = slice(128 + h * HD, 128 + (h + 1) * HD)
            s = dot(k2, padded(qd_t[krows, span(i)], h)) + bias[i, WIN:KEYS]
            top_w = top_win[head]
            top = jnp.maximum(jnp.max(s, axis=0, keepdims=True), top_w)
            e = jnp.exp(s - top)
            scale_w = jnp.exp(top_w - top)
            inv_total = 1.0 / (jnp.sum(e, axis=0, keepdims=True) + sum_win[head] * scale_w)
            prob_l = e * inv_total
            prob_w = e_win[head] * (scale_w * inv_total)
            low_l = prob_l.astype(BF16)
            low_w = prob_w.astype(BF16)
            low_win[head] = low_w
            mixed = dot(kv_t[vrows, win], low_w) + dot(lkv_t[i, vrows, :], low_l)
            mixes.append(mixed)
            dot_t = qd_t[vrows, span(i)]
            delta = jnp.sum(dot_t.astype(F32) * mixed, axis=0, keepdims=True)
            dot_w = padded(dot_t, h)
            ds_l = (prob_l * (dot(v2, dot_w) - delta)).astype(BF16)
            ds_w = (prob_w * (dot(v2w, dot_w) - delta)).astype(BF16)
            ds_win[head] = ds_w
            dqs.append((dot(kv_t[krows, win], ds_w) + dot(lkv_t[i, krows, :], ds_l)) * 0.125)
            dk2 = dk2 + dot(ds_l, halved(q2, h))
            dv2 = dv2 + dot(low_l, halved(do2, h))
        for j in range(NLAND):
            at = slice(j * BLK, (j + 1) * BLK)
            g_land[i, j, :, 0:128] = dk2[at]
            g_land[i, j, :, 128:256] = dv2[at]
        valid = jnp.zeros((1, ROWS), jnp.bool_)
        for b in range(PC):
            valid = valid | ((lanes >= b * BLK) & (lanes < b * BLK + counts_ref[b, 4 * z + i]))
        o_tx[i, :, 0:128] = jnp.where(valid, jnp.concatenate(mixes, axis=0), 0.0).T.astype(BF16)
        o_tx[i, :, 128:256] = jnp.concatenate(dqs, axis=0).T.astype(BF16)

    def o_to(i):
        return remote(o_tx.at[i], o_rx.at[p], o_s.at[i], o_r.at[p], 4 * z + i)

    def o_from(i):
        return remote(o_tx.at[i], o_rx.at[i], o_s.at[i], o_r.at[i], 4 * z + i)

    def send_outputs(i):
        pl.when(p != i)(lambda: o_to(i).start())

        @pl.when(p == i)
        def _():
            o_rx[i] = o_tx[i]

    touched = set()

    def edge_up():
        return remote(edge_tx.at[0], edge_rx.at[0], edge_s.at[0], edge_r.at[0], me + 4)

    def edge_dn():
        return remote(edge_tx.at[1], edge_rx.at[1], edge_s.at[1], edge_r.at[1], me - 4)

    def window_grads(i):
        q2 = qd[span(i), 0:128]
        do2 = qd[span(i), 128:256]
        dk2 = dot(ds_win[2 * i], halved(q2, 0)) + dot(ds_win[2 * i + 1], halved(q2, 1))
        dv2 = dot(low_win[2 * i], halved(do2, 0)) + dot(low_win[2 * i + 1], halved(do2, 1))
        for term, at in ((dk2, slice(0, 128)), (dv2, slice(128, 256))):
            for a in range(3):
                piece = term[span(a)]
                if i + a == 0:
                    edge_tx[1, :, at] = piece.astype(BF16)
                elif i + a == 5:
                    edge_tx[0, :, at] = piece.astype(BF16)
                elif (i + a, at.start) in touched:
                    grads[span(i + a), at] = grads[span(i + a), at] + piece
                else:
                    touched.add((i + a, at.start))
                    grads[span(i + a), at] = piece
        if i == 0:
            pl.when(z > 0)(lambda: edge_dn().start())
        if i == 3:
            pl.when(z < last)(lambda: edge_up().start())

    def g_to(i):
        return remote(g_tx.at[i], g_rx.at[p], g_s.at[i], g_r.at[p], 4 * z + i)

    def g_from(i):
        return remote(g_tx.at[i], g_rx.at[i], g_s.at[i], g_r.at[i], 4 * z + i)

    def send_grads(i):
        if i == 0:

            @pl.when(z > 0)
            def _():
                edge_up().wait_recv()
                grads[span(1)] = grads[span(1)] + edge_rx[0].astype(F32)

        if i == 3:

            @pl.when(z < last)
            def _():
                edge_dn().wait_recv()
                grads[span(4)] = grads[span(4)] + edge_rx[1].astype(F32)

        g_tx[i] = grads[span(1 + i)].astype(BF16)
        pl.when(p != i)(lambda: g_to(i).start())

        @pl.when(p == i)
        def _():
            g_rx[i] = g_tx[i]

    def slot_of(i, row):
        found = NLAND
        for j in range(NLAND):
            found = jnp.where(rows_quad[i, 0, j] == row, j, found)
        return found

    def gathered(row):
        return sum(g_land[i, slot_of(i, row)] for i in quad)

    def relay(zz, way):
        return remote(
            part_tx.at[zz], relay_rx.at[zz], relay_s.at[zz], relay_r.at[zz], me - 4 * way
        )

    def to_owner(zz, way, s):
        code = (0 if way > 0 else 2) + s - 1
        return remote(
            part_tx.at[zz], owner_rx.at[code], owner_s.at[code], owner_r.at[code], me - 4 * way * s
        )

    def reduce_step(s):
        def step(zz, way, more):
            for t in quad:
                part[t] = gathered(4 * zz + t)
            if s >= 2:

                @pl.when(more)
                def _():
                    relay(zz, way).wait_recv()
                    part[...] = part[...] + relay_rx[zz].astype(F32)

            part_tx[zz] = part[...].astype(BF16)
            if s >= 3:
                relay(zz, way).start()
            else:
                to_owner(zz, way, s).start()

        each_side(s, step)

    def reduce_own():
        for t in quad:
            total[t] = gathered(4 * z + t)

    def total_to(t):
        return remote(total_tx.at[t], total_rx.at[p], total_s.at[t], total_r.at[p], 4 * z + t)

    def total_from(t):
        return remote(total_tx.at[t], total_rx.at[t], total_s.at[t], total_r.at[t], 4 * z + t)

    def reduce_finish():
        for s in (1, 2):
            for way in (1, -1):
                exists = z + s <= last if way > 0 else z - s >= 0

                @pl.when(exists)
                def _():
                    to_owner(z, way, s).wait_recv()
                    code = (0 if way > 0 else 2) + s - 1
                    total[...] = total[...] + owner_rx[code].astype(F32)

        total_tx[...] = total[...].astype(BF16)
        for t in quad:
            pl.when(p != t)(lambda: total_to(t).start())

            @pl.when(p == t)
            def _():
                total_rx[t] = total_tx[t]

    def write_outputs():
        others(lambda i: o_from(i).wait_recv())
        for i in quad:
            attn_ref[:, cols(i)] = o_rx[i, :, 0:128]
            qgrad_ref[:, cols(i)] = o_rx[i, :, 128:256]

    def write_grads():
        others(lambda i: g_from(i).wait_recv())
        others(lambda i: total_from(i).wait_recv())
        for i in quad:
            for b in range(PC):
                at = slice(b * BLK, (b + 1) * BLK)
                hit = own_col == b
                both = g_rx[i, at].astype(F32) + jnp.where(hit, total_rx[i].astype(F32), 0.0)
                kgrad_ref[at, cols(i)] = both[:, 0:128].astype(BF16)
                vgrad_ref[at, cols(i)] = both[:, 128:256].astype(BF16)

    def gather_sent():
        others(lambda i: rows_to(i).wait_send())
        others(lambda i: land_to(i).wait_send())
        others(lambda i: kv_to(i).wait_send())
        others(lambda i: qd_to(i).wait_send())
        panel_own(lambda copy: copy.wait_send())
        for s in range(2, last):
            each_side(
                s, lambda zz, way, more: pl.when(more)(lambda: panel_to(zz, way).wait_send())
            )
        pl.when(z < last)(lambda: halo_up().wait_send())
        pl.when(z > 0)(lambda: halo_dn().wait_send())

    def reduce_sent():
        others(lambda i: o_to(i).wait_send())
        others(lambda i: g_to(i).wait_send())
        pl.when(z < last)(lambda: edge_up().wait_send())
        pl.when(z > 0)(lambda: edge_dn().wait_send())
        for s in range(1, last + 1):

            def step(zz, way, more):
                (relay(zz, way) if s >= 3 else to_owner(zz, way, s)).wait_send()

            each_side(s, step)
        others(lambda t: total_to(t).wait_send())

    others(lambda i: land_to(i).start())
    others(lambda i: rows_to(i).start())
    others(lambda i: kv_to(i).start())
    panel[me] = land_tx[p]
    kv[dyn_span(1 + p)] = kv_tx[p]
    set_queries()
    others(lambda i: qd_to(i).start())
    qd[dyn_span(p)] = qd_tx[p]
    for i in quad:
        g_land[i, NLAND] = jnp.zeros((BLK, 256), F32)
    window_bias(0)
    others(lambda i: land_from(i).wait_recv())
    panel_own(lambda copy: copy.start())
    for i in (1, 2, 3):
        window_bias(i)
    take_rows()
    others(lambda i: kv_from(i).wait_recv())
    pl.when(z < last)(lambda: halo_up().start())
    pl.when(z > 0)(lambda: halo_dn().start())
    for i in quad:
        turn(1 + i)
    others(lambda i: qd_from(i).wait_recv())
    for i in quad:
        turn_queries(i)
    window_scores(1)
    for s in range(2, last + 1):
        panel_relay(s)
    window_scores(2)
    pl.when(z > 0)(lambda: halo_up().wait_recv())
    pl.when(z < last)(lambda: halo_dn().wait_recv())
    turn(0)
    turn(5)
    window_scores(0)
    window_scores(3)
    panel_near()
    for i in (0, 3, 1, 2):
        take_landmarks(i)
        landmarks(i)
        send_outputs(i)
    for s in range(last, 0, -1):
        reduce_step(s)
        if s == last:
            window_grads(0)
            window_grads(3)
    if last == 0:
        window_grads(0)
        window_grads(3)
    window_grads(1)
    window_grads(2)
    send_grads(1)
    send_grads(2)
    reduce_own()
    send_grads(0)
    send_grads(3)
    gather_sent()
    write_outputs()
    reduce_finish()
    write_grads()
    reduce_sent()


def emit_kernel(*refs):
    for source, result in zip(refs[:4], refs[4:]):
        result[...] = source[...]


VM = pl.BlockSpec(memory_space=pltpu.VMEM)
SM = pl.BlockSpec(memory_space=pltpu.SMEM)
DMA = pltpu.SemaphoreType.DMA


def shape(dims, dtype):
    return jax.ShapeDtypeStruct(dims, dtype)


def per_device(n, queries, keys, values, out_grad, valid_counts, landmark_cols, landmark_rows):
    depth = n // 4
    flat = (ROWS, WIDTH)
    block_rows = (PC, BLK, WIDTH)
    quad_rows = (4, ROWS, 256)
    quad_blocks = (4, BLK, 256)
    vmem = pltpu.VMEM
    results = pl.pallas_call(
        functools.partial(fused_kernel, n),
        out_shape=[shape(flat, BF16)] * 4,
        in_specs=[SM] * 3 + [VM] * 4,
        out_specs=[VM] * 4,
        scratch_shapes=[
            vmem((8, 128), jnp.int32),
            vmem((4, 8, 128), jnp.int32),
            pltpu.SMEM((4, 8, 128), jnp.int32),
            vmem(quad_blocks, BF16),
            vmem(quad_rows, BF16),
            vmem(quad_rows, BF16),
            vmem((n, BLK, 256), BF16),
            vmem((6 * ROWS, 256), BF16),
            vmem((256, 6 * ROWS), BF16),
            vmem((4 * ROWS, 256), BF16),
            vmem((256, 4 * ROWS), BF16),
            vmem((4, NLAND * BLK, 256), BF16),
            vmem((4, 256, NLAND * BLK), BF16),
            vmem((4, KEYS, ROWS), F32),
            vmem((HEADS, WIN, ROWS), F32),
            vmem((HEADS, 1, ROWS), F32),
            vmem((HEADS, 1, ROWS), F32),
            vmem((HEADS, WIN, ROWS), BF16),
            vmem((HEADS, WIN, ROWS), BF16),
            vmem((6 * ROWS, 256), F32),
            vmem((4, NLAND + 1, BLK, 256), F32),
            vmem(quad_rows, BF16),
            vmem(quad_rows, BF16),
            vmem((2, ROWS, 256), BF16),
            vmem((2, ROWS, 256), BF16),
            vmem(quad_rows, BF16),
            vmem(quad_rows, BF16),
            vmem(quad_blocks, F32),
            vmem((depth,) + quad_blocks, BF16),
            vmem((depth,) + quad_blocks, BF16),
            vmem((4,) + quad_blocks, BF16),
            vmem(quad_blocks, F32),
            vmem(quad_blocks, BF16),
            vmem(quad_blocks, BF16),
            DMA((1,)),
            DMA((4,)),
            DMA((4,)),
            DMA((4,)),
            DMA((4,)),
            DMA((4,)),
            DMA((4,)),
            DMA((4,)),
            DMA((4,)),
            DMA((depth,)),
            DMA((depth,)),
            DMA((2,)),
            DMA((depth,)),
            DMA((2,)),
            DMA((2,)),
            DMA((4,)),
            DMA((4,)),
            DMA((2,)),
            DMA((2,)),
            DMA((4,)),
            DMA((4,)),
            DMA((depth,)),
            DMA((depth,)),
            DMA((4,)),
            DMA((4,)),
            DMA((4,)),
            DMA((4,)),
        ],
        compiler_params=pltpu.CompilerParams(
            collective_id=0, has_side_effects=True, vmem_limit_bytes=VMEM_LIMIT
        ),
    )(
        landmark_cols,
        landmark_rows,
        valid_counts.T,
        queries,
        keys.reshape(block_rows),
        values.reshape(block_rows),
        out_grad,
    )
    return tuple(
        pl.pallas_call(
            emit_kernel,
            out_shape=[shape(flat, BF16)] * 4,
            in_specs=[VM] * 4,
            out_specs=[VM] * 4,
        )(*results)
    )


def solution(mesh):
    n = mesh.shape["prow"]
    tokens = P(("chars", "prow"), None)
    return jax.shard_map(
        functools.partial(per_device, n),
        mesh=mesh,
        in_specs=(tokens, tokens, tokens, tokens, P("chars", None), P("chars"), tokens),
        out_specs=(tokens, tokens, tokens, tokens),
        check_vma=False,
    )
```

```python
import functools

import jax
import jax.numpy as jnp
from jax import lax
from jax.experimental import pallas as pl
from jax.experimental.pallas import tpu as pltpu
from jax.sharding import PartitionSpec as P

HEADS = 8
HD = 64
BLK = 64
NLAND = 4
PC = 4
WIDTH = HEADS * HD
ROWS = PC * BLK
KEYS = 3 * ROWS + NLAND * BLK
F32 = jnp.float32
BF16 = jnp.bfloat16
MESH = pl.DeviceIdType.MESH
masked_score = -1e30
WIN = 3 * ROWS
VMEM_LIMIT = 60 * 1024 * 1024


def dot(a, b):
    return lax.dot_general(a, b, (((1,), (0,)), ((), ())), preferred_element_type=F32)


def remote(src, dst, send, recv, device):
    return pltpu.make_async_remote_copy(
        src_ref=src,
        dst_ref=dst,
        send_sem=send,
        recv_sem=recv,
        device_id={"prow": device},
        device_id_type=MESH,
    )


def position():
    me = lax.axis_index("prow")
    return me, me // 4, me % 4


def neighbours(n):
    me, z, p = position()
    last = n // 4 - 1
    found = [(4 * z + i, p != i) for i in range(4)]
    for step in (1, 2):
        found.append((me + 4 * step, z + step <= last))
        found.append((me - 4 * step, z - step >= 0))
    return found


def greet(n):
    barrier = pltpu.get_barrier_semaphore()
    for device, exists in neighbours(n):

        @pl.when(exists)
        def _():
            pl.semaphore_signal(barrier, inc=1, device_id={"prow": device}, device_id_type=MESH)


def met(n):
    count = 0
    for _, exists in neighbours(n):
        count = count + jnp.where(exists, 1, 0)
    pl.semaphore_wait(pltpu.get_barrier_semaphore(), count)


def fused_kernel(
    n,
    cols_ref,
    rows_ref,
    counts_ref,
    q_in,
    k_in,
    v_in,
    do_in,
    attn_out,
    qgrad_out,
    kgrad_out,
    vgrad_out,
    kland_out,
    vland_out,
    q_ref,
    k_ref,
    v_ref,
    do_ref,
    rows_tx,
    rows_rx,
    rows_quad,
    land_tx,
    kv_tx,
    qd_tx,
    panel,
    kv,
    kv_t,
    qd,
    qd_t,
    lkv,
    lkv_t,
    bias,
    e_win,
    top_win,
    sum_win,
    scale_win,
    delta_win,
    low_win,
    ds_win,
    ds_land,
    grads,
    g_land,
    o_tx,
    edge_tx,
    edge_rx,
    g_tx,
    part,
    part_tx,
    relay_rx,
    owner_rx,
    total,
    total_tx,
    load_s,
    local_sem,
    own_s,
    rows_s,
    rows_r,
    land_s,
    land_r,
    kv_s,
    kv_r,
    qd_s,
    qd_r,
    panel_up,
    panel_dn,
    panel_far,
    panel_r,
    halo_s,
    halo_r,
    o_s,
    o_r,
    edge_s,
    edge_r,
    g_s,
    g_r,
    relay_s,
    relay_r,
    owner_s,
    owner_r,
    total_s,
    total_r,
):
    me, z, p = position()
    depth = n // 4
    last = depth - 1
    quad = range(4)
    own_col = cols_ref[me]
    greet(n)
    loads = [
        pltpu.make_async_copy(source, place, load_s.at[at])
        for at, (source, place) in enumerate(
            ((k_in, k_ref), (v_in, v_ref), (q_in, q_ref), (do_in, do_ref))
        )
    ]
    for copy in loads:
        copy.start()

    def span(i):
        return slice(i * ROWS, (i + 1) * ROWS)

    def dyn_span(i):
        return pl.ds(pl.multiple_of(i * ROWS, ROWS), ROWS)

    def cols(i):
        return slice(i * 128, (i + 1) * 128)

    loads[0].wait()
    loads[1].wait()
    k_own = k_ref[own_col]
    v_own = v_ref[own_col]
    lane = lax.broadcasted_iota(jnp.int32, (8, 128), 1)
    ints = jnp.zeros((8, 128), jnp.int32)
    for j in range(NLAND):
        ints = jnp.where(lane == j, rows_ref[0, j], ints)
    rows_tx[...] = ints
    rows_rx[p] = ints
    k_rows = k_ref[...].reshape(ROWS, WIDTH)
    v_rows = v_ref[...].reshape(ROWS, WIDTH)
    for i in quad:
        land_tx[i, :, :128] = k_own[:, cols(i)]
        land_tx[i, :, 128:] = v_own[:, cols(i)]
        kv_tx[i, :, :128] = k_rows[:, cols(i)]
        kv_tx[i, :, 128:] = v_rows[:, cols(i)]

    @pl.when(z == 0)
    def _():
        kv[span(0)] = jnp.zeros((ROWS, 256), BF16)

    @pl.when(z == last)
    def _():
        kv[span(5)] = jnp.zeros((ROWS, 256), BF16)

    met(n)

    def rows_to(i):
        return remote(rows_tx, rows_rx.at[p], rows_s.at[i], rows_r.at[p], 4 * z + i)

    def rows_from(i):
        return remote(rows_tx, rows_rx.at[i], rows_s.at[i], rows_r.at[i], 4 * z + i)

    def land_to(i):
        return remote(land_tx.at[i], panel.at[me], land_s.at[i], land_r.at[p], 4 * z + i)

    def land_from(i):
        return remote(land_tx.at[i], panel.at[4 * z + i], land_s.at[i], land_r.at[i], 4 * z + i)

    def kv_to(i):
        return remote(kv_tx.at[i], kv.at[dyn_span(1 + p)], kv_s.at[i], kv_r.at[p], 4 * z + i)

    def kv_from(i):
        return remote(kv_tx.at[i], kv.at[span(1 + i)], kv_s.at[i], kv_r.at[i], 4 * z + i)

    def qd_to(i):
        return remote(qd_tx.at[i], qd.at[dyn_span(p)], qd_s.at[i], qd_r.at[p], 4 * z + i)

    def qd_from(i):
        return remote(qd_tx.at[i], qd.at[span(i)], qd_s.at[i], qd_r.at[i], 4 * z + i)

    def others(act):
        for i in quad:
            pl.when(p != i)(lambda: act(i))

    def panel_to(zz, h, step):
        place = panel.at[pl.ds(4 * zz + 2 * h, 2)]
        if step == 1:
            send = panel_up.at[zz, h]
        elif step == -1:
            send = panel_dn.at[zz, h]
        else:
            send = panel_far.at[0 if step > 0 else 1, h]
        return remote(place, place, send, panel_r.at[zz, h], me + 4 * step)

    def panel_own(h, act):
        for step in (2, -2, 1, -1):
            exists = z + step <= last if step > 0 else z + step >= 0
            pl.when(exists)(lambda: act(panel_to(z, h, step)))

    def each_side(s, act):
        pl.when(z - s >= 0)(lambda: act(z - s, 1, z < last))
        pl.when(z + s <= last)(lambda: act(z + s, -1, z > 0))

    def panel_relay(s, h):
        def step(zz, way, more):
            panel_to(zz, h, way).wait_recv()
            pl.when(more)(lambda: panel_to(zz, h, way).start())

        each_side(s, step)

    def panel_wait(s):
        for h in range(2):
            each_side(s, lambda zz, way, more: panel_to(zz, h, way).wait_recv())

    def halo_up():
        return remote(kv.at[span(4)], kv.at[span(0)], halo_s.at[0], halo_r.at[0], me + 4)

    def halo_dn():
        return remote(kv.at[span(1)], kv.at[span(5)], halo_s.at[1], halo_r.at[1], me - 4)

    pos = lax.broadcasted_iota(jnp.int32, (BLK, ROWS), 0)
    qcol = lax.broadcasted_iota(jnp.int32, (BLK, ROWS), 1) // BLK

    def window_bias(i):
        for a in range(3):
            row = 4 * z + i + a - 1
            inside = jnp.logical_and(row >= 0, row < n)
            safe = jnp.clip(row, 0, n - 1)
            for b in range(PC):
                count = jnp.where(inside, counts_ref[b, safe], 0)
                ok = (pos < count) & (qcol >= b - 1) & (qcol <= b + 1)
                base = a * ROWS + b * BLK
                bias[i, base : base + BLK] = jnp.where(ok, 0.0, masked_score)

    def set_queries():
        loads[2].wait()
        loads[3].wait()
        tpos = lax.broadcasted_iota(jnp.int32, (BLK, WIDTH), 0)
        for b in range(PC):
            at = slice(b * BLK, (b + 1) * BLK)
            part_q = q_ref[at] * 0.125
            part_d = do_ref[at].astype(F32)
            part_d = jnp.where(tpos < counts_ref[b, me], part_d, 0.0).astype(BF16)
            for i in quad:
                qd_tx[i, at, :128] = part_q[:, cols(i)]
                qd_tx[i, at, 128:] = part_d[:, cols(i)]

    def turn(a):
        kv_t[:, span(a)] = kv[span(a)].T

    def turn_queries(i):
        qd_t[:, span(i)] = qd[span(i)].T

    def take_rows():
        others(lambda i: rows_from(i).wait_recv())
        copy = pltpu.make_async_copy(rows_rx, rows_quad, local_sem.at[0])
        copy.start()
        copy.wait()

    def take_landmarks(i):
        for j in range(NLAND):
            row = rows_quad[i, 0, j]
            count = counts_ref[cols_ref[row], row]
            base = WIN + j * BLK
            bias[i, base : base + BLK] = jnp.where(pos < count, 0.0, masked_score)
            block = panel[row]
            at = slice(j * BLK, (j + 1) * BLK)
            lkv[i, at] = block
            lkv_t[i, :, at] = block.T

    zero = jnp.zeros((HD, ROWS), BF16)

    def padded(rows_t, h):
        return jnp.concatenate([rows_t, zero] if h == 0 else [zero, rows_t], axis=0)

    def window_scores(i):
        k2 = kv[i * ROWS : i * ROWS + WIN, 0:128]
        for h in range(2):
            head = 2 * i + h
            s = dot(k2, padded(qd_t[h * HD : (h + 1) * HD, span(i)], h)) + bias[i, 0:WIN]
            top = jnp.max(s, axis=0, keepdims=True)
            e = jnp.exp(s - top)
            e_win[head] = e
            top_win[head] = top
            sum_win[head] = jnp.sum(e, axis=0, keepdims=True)

    left = lax.broadcasted_iota(jnp.int32, (ROWS, 128), 1) < HD

    def halved(block, h):
        keep = left if h == 0 else jnp.logical_not(left)
        return jnp.where(keep, block.astype(F32), 0.0).astype(BF16)

    lanes = lax.broadcasted_iota(jnp.int32, (1, ROWS), 1)

    def queries_of(i):
        return qd[span(i), 0:128], qd[span(i), 128:256]

    def landmarks(i):
        win = slice(i * ROWS, i * ROWS + WIN)
        k2 = lkv[i, :, 0:128]
        v2 = lkv[i, :, 128:256]
        q2, do2 = queries_of(i)
        dk2 = 0.0
        dv2 = 0.0
        mixes = []
        for h in range(2):
            head = 2 * i + h
            krows = slice(h * HD, (h + 1) * HD)
            vrows = slice(128 + h * HD, 128 + (h + 1) * HD)
            s = dot(k2, padded(qd_t[krows, span(i)], h)) + bias[i, WIN:KEYS]
            top_w = top_win[head]
            top = jnp.maximum(jnp.max(s, axis=0, keepdims=True), top_w)
            e = jnp.exp(s - top)
            scale_w = jnp.exp(top_w - top)
            inv_total = 1.0 / (jnp.sum(e, axis=0, keepdims=True) + sum_win[head] * scale_w)
            prob_l = e * inv_total
            scale_w = scale_w * inv_total
            low_l = prob_l.astype(BF16)
            low_w = (e_win[head] * scale_w).astype(BF16)
            low_win[head] = low_w
            mixed = dot(kv_t[vrows, win], low_w) + dot(lkv_t[i, vrows, :], low_l)
            mixes.append(mixed)
            dot_t = qd_t[vrows, span(i)]
            delta = jnp.sum(dot_t.astype(F32) * mixed, axis=0, keepdims=True)
            scale_win[head] = scale_w
            delta_win[head] = delta
            ds_l = (prob_l * (dot(v2, padded(dot_t, h)) - delta)).astype(BF16)
            ds_land[head] = ds_l
            dk2 = dk2 + dot(ds_l, halved(q2, h))
            dv2 = dv2 + dot(low_l, halved(do2, h))
        for j in range(NLAND):
            at = slice(j * BLK, (j + 1) * BLK)
            g_land[i, j, :, 0:128] = dk2[at]
            g_land[i, j, :, 128:256] = dv2[at]
        valid = jnp.zeros((1, ROWS), jnp.bool_)
        for b in range(PC):
            valid = valid | ((lanes >= b * BLK) & (lanes < b * BLK + counts_ref[b, 4 * z + i]))
        mixed = jnp.where(valid, jnp.concatenate(mixes, axis=0), 0.0)
        send_output(0, i, mixed.T.astype(BF16))

    def window_scores_grad(i):
        win = slice(i * ROWS, i * ROWS + WIN)
        v2w = kv[win, 128:256]
        dqs = []
        for h in range(2):
            head = 2 * i + h
            krows = slice(h * HD, (h + 1) * HD)
            vrows = slice(128 + h * HD, 128 + (h + 1) * HD)
            prob_w = e_win[head] * scale_win[head]
            dot_w = padded(qd_t[vrows, span(i)], h)
            ds_w = (prob_w * (dot(v2w, dot_w) - delta_win[head])).astype(BF16)
            ds_win[head] = ds_w
            dqs.append(
                (dot(kv_t[krows, win], ds_w) + dot(lkv_t[i, krows, :], ds_land[head])) * 0.125
            )
        send_output(1, i, jnp.concatenate(dqs, axis=0).T.astype(BF16))

    my_cols = pl.ds(pl.multiple_of(p * 128, 128), 128)

    def piece_to(at, src, out, sends, recvs, i):
        return remote(src, out.at[:, my_cols], sends.at[at, i], recvs.at[at, p], 4 * z + i)

    def piece_from(at, src, out, sends, recvs, i):
        return remote(src, out.at[:, cols(i)], sends.at[at, i], recvs.at[at, i], 4 * z + i)

    def piece_own(at, src, out, i):
        return pltpu.make_async_copy(src, out.at[:, cols(i)], own_s.at[at])

    def deliver(at, src, out, sends, recvs, i):
        pl.when(p != i)(lambda: piece_to(at % 2, src, out, sends, recvs, i).start())
        pl.when(p == i)(lambda: piece_own(at, src, out, i).start())

    def delivered(at, srcs, out, sends, recvs):
        for i in quad:
            src = srcs.at[at % 2, i]

            @pl.when(p != i)
            def _():
                piece_from(at % 2, src, out, sends, recvs, i).wait_recv()

            pl.when(p == i)(lambda: piece_own(at, src, out, i).wait())

    def sent(at, srcs, out, sends, recvs):
        for i in quad:
            src = srcs.at[at % 2, i]
            pl.when(p != i)(
                lambda: piece_to(at % 2, src, out, sends, recvs, i).wait_send()
            )

    out_plan = (
        (0, o_tx, attn_out, o_s, o_r),
        (1, o_tx, qgrad_out, o_s, o_r),
        (2, g_tx, kgrad_out, g_s, g_r),
        (3, g_tx, vgrad_out, g_s, g_r),
        (4, total_tx, kland_out, total_s, total_r),
        (5, total_tx, vland_out, total_s, total_r),
    )

    def send_piece(at, i):
        _, srcs, out, sends, recvs = out_plan[at]
        deliver(at, srcs.at[at % 2, i], out, sends, recvs, i)

    def send_output(f, i, rows):
        o_tx[f, i] = rows
        send_piece(f, i)

    touched = set()

    def edge_up():
        return remote(edge_tx.at[0], edge_rx.at[0], edge_s.at[0], edge_r.at[0], me + 4)

    def edge_dn():
        return remote(edge_tx.at[1], edge_rx.at[1], edge_s.at[1], edge_r.at[1], me - 4)

    def window_grads(i):
        q2, do2 = queries_of(i)
        dk2 = dot(ds_win[2 * i], halved(q2, 0)) + dot(ds_win[2 * i + 1], halved(q2, 1))
        dv2 = dot(low_win[2 * i], halved(do2, 0)) + dot(low_win[2 * i + 1], halved(do2, 1))
        for term, at in ((dk2, slice(0, 128)), (dv2, slice(128, 256))):
            for a in range(3):
                piece = term[span(a)]
                if i + a == 0:
                    edge_tx[1, :, at] = piece.astype(BF16)
                elif i + a == 5:
                    edge_tx[0, :, at] = piece.astype(BF16)
                elif (i + a, at.start) in touched:
                    grads[span(i + a), at] = grads[span(i + a), at] + piece
                else:
                    touched.add((i + a, at.start))
                    grads[span(i + a), at] = piece
        if i == 0:
            pl.when(z > 0)(lambda: edge_dn().start())
        if i == 3:
            pl.when(z < last)(lambda: edge_up().start())

    def send_grads(i):
        if i == 0:

            @pl.when(z > 0)
            def _():
                edge_up().wait_recv()
                grads[span(1)] = grads[span(1)] + edge_rx[0].astype(F32)

        if i == 3:

            @pl.when(z < last)
            def _():
                edge_dn().wait_recv()
                grads[span(4)] = grads[span(4)] + edge_rx[1].astype(F32)

        both = grads[span(1 + i)].astype(BF16)
        for f in range(2):
            g_tx[f, i] = both[:, cols(f)]
            send_piece(2 + f, i)

    def slot_of(i, row):
        found = NLAND
        for j in range(NLAND):
            found = jnp.where(rows_quad[i, 0, j] == row, j, found)
        return found

    def gathered(row):
        return sum(g_land[i, slot_of(i, row)] for i in quad)

    def relay(zz, way):
        return remote(
            part_tx.at[zz], relay_rx.at[zz], relay_s.at[zz], relay_r.at[zz], me - 4 * way
        )

    def to_owner(zz, way, s):
        code = (0 if way > 0 else 2) + s - 1
        return remote(
            part_tx.at[zz], owner_rx.at[code], owner_s.at[code], owner_r.at[code], me - 4 * way * s
        )

    def reduce_step(s):
        def step(zz, way, more):
            for t in quad:
                part[t] = gathered(4 * zz + t)
            if s >= 2:

                @pl.when(more)
                def _():
                    relay(zz, way).wait_recv()
                    part[...] = part[...] + relay_rx[zz].astype(F32)

            part_tx[zz] = part[...].astype(BF16)
            if s >= 3:
                relay(zz, way).start()
            else:
                to_owner(zz, way, s).start()

        each_side(s, step)

    def reduce_own():
        for t in quad:
            total[t] = gathered(4 * z + t)

    def reduce_finish():
        for s in (1, 2):
            for way in (1, -1):
                exists = z + s <= last if way > 0 else z - s >= 0

                @pl.when(exists)
                def _():
                    to_owner(z, way, s).wait_recv()
                    code = (0 if way > 0 else 2) + s - 1
                    total[...] = total[...] + owner_rx[code].astype(F32)

        for f in range(2):
            for t in quad:
                total_tx[f, t] = total[t, :, cols(f)].astype(BF16)
                send_piece(4 + f, t)

    def outputs_done():
        for plan in out_plan:
            delivered(*plan)

    def gather_sent():
        others(lambda i: rows_to(i).wait_send())
        others(lambda i: land_to(i).wait_send())
        others(lambda i: kv_to(i).wait_send())
        others(lambda i: qd_to(i).wait_send())
        for h in range(2):
            panel_own(h, lambda copy: copy.wait_send())
            for s in range(2, last):
                each_side(
                    s,
                    lambda zz, way, more: pl.when(more)(
                        lambda: panel_to(zz, h, way).wait_send()
                    ),
                )
        pl.when(z < last)(lambda: halo_up().wait_send())
        pl.when(z > 0)(lambda: halo_dn().wait_send())

    def reduce_sent():
        pl.when(z < last)(lambda: edge_up().wait_send())
        pl.when(z > 0)(lambda: edge_dn().wait_send())
        for s in range(1, last + 1):

            def step(zz, way, more):
                (relay(zz, way) if s >= 3 else to_owner(zz, way, s)).wait_send()

            each_side(s, step)
        for plan in out_plan:
            sent(*plan)

    others(lambda i: land_to(i).start())
    others(lambda i: kv_to(i).start())
    others(lambda i: rows_to(i).start())
    panel[me] = land_tx[p]
    y = p // 2
    for i in quad:
        pl.when(jnp.logical_and(i // 2 == y, i != p))(lambda: land_from(i).wait_recv())
    panel_own(y, lambda copy: copy.start())
    kv[dyn_span(1 + p)] = kv_tx[p]
    set_queries()
    others(lambda i: qd_to(i).start())
    qd[dyn_span(p)] = qd_tx[p]
    for i in quad:
        pl.when(i // 2 != y)(lambda: land_from(i).wait_recv())
    panel_own(1 - y, lambda copy: copy.start())
    for i in quad:
        g_land[i, NLAND] = jnp.zeros((BLK, 256), F32)
        window_bias(i)
    for s in range(2, last):
        panel_relay(s, y)
        panel_relay(s, 1 - y)
    others(lambda i: kv_from(i).wait_recv())
    pl.when(z < last)(lambda: halo_up().start())
    pl.when(z > 0)(lambda: halo_dn().start())
    for i in quad:
        turn(1 + i)
    take_rows()
    others(lambda i: qd_from(i).wait_recv())
    for i in quad:
        turn_queries(i)
    window_scores(1)
    window_scores(2)
    pl.when(z > 0)(lambda: halo_up().wait_recv())
    pl.when(z < last)(lambda: halo_dn().wait_recv())
    turn(0)
    turn(5)
    window_scores(0)
    window_scores(3)
    for s in sorted({1, last} - {0}):
        panel_wait(s)
    for i in quad:
        take_landmarks(i)
        landmarks(i)
    for s in range(last, 2, -1):
        reduce_step(s)
    if last > 0:
        reduce_step(1)
    for i in (0, 3):
        window_scores_grad(i)
        window_grads(i)
    if last > 1:
        reduce_step(2)
    for i in (1, 2):
        window_scores_grad(i)
        window_grads(i)
    send_grads(1)
    send_grads(2)
    reduce_own()
    send_grads(0)
    send_grads(3)
    gather_sent()
    reduce_finish()
    reduce_sent()
    outputs_done()


def emit_kernel(cols_ref, attn, qgrad, kgrad, vgrad, kland, vland, *results):
    own_col = cols_ref[lax.axis_index("prow")]
    results[0][...] = attn[...]
    results[1][...] = qgrad[...]
    for source, land, result in ((kgrad, kland, results[2]), (vgrad, vland, results[3])):
        term = land[...].astype(F32)
        for b in range(PC):
            at = slice(b * BLK, (b + 1) * BLK)
            result[at] = (source[at].astype(F32) + jnp.where(own_col == b, term, 0.0)).astype(BF16)


VM = pl.BlockSpec(memory_space=pltpu.VMEM)
SM = pl.BlockSpec(memory_space=pltpu.SMEM)
ANY = pl.BlockSpec(memory_space=pl.ANY)
DMA = pltpu.SemaphoreType.DMA


def shape(dims, dtype):
    return jax.ShapeDtypeStruct(dims, dtype)


def per_device(n, queries, keys, values, out_grad, valid_counts, landmark_cols, landmark_rows):
    depth = n // 4
    flat = (ROWS, WIDTH)
    block_rows = (PC, BLK, WIDTH)
    quad_rows = (4, ROWS, 256)
    quad_blocks = (4, BLK, 256)
    vmem = pltpu.VMEM
    results = pl.pallas_call(
        functools.partial(fused_kernel, n),
        out_shape=[shape(flat, BF16)] * 4 + [shape((BLK, WIDTH), BF16)] * 2,
        in_specs=[SM] * 3 + [ANY] * 4,
        out_specs=[ANY] * 6,
        scratch_shapes=[
            vmem(flat, BF16),
            vmem(block_rows, BF16),
            vmem(block_rows, BF16),
            vmem(flat, BF16),
            vmem((8, 128), jnp.int32),
            vmem((4, 8, 128), jnp.int32),
            pltpu.SMEM((4, 8, 128), jnp.int32),
            vmem(quad_blocks, BF16),
            vmem(quad_rows, BF16),
            vmem(quad_rows, BF16),
            vmem((n, BLK, 256), BF16),
            vmem((6 * ROWS, 256), BF16),
            vmem((256, 6 * ROWS), BF16),
            vmem((4 * ROWS, 256), BF16),
            vmem((256, 4 * ROWS), BF16),
            vmem((4, NLAND * BLK, 256), BF16),
            vmem((4, 256, NLAND * BLK), BF16),
            vmem((4, KEYS, ROWS), F32),
            vmem((HEADS, WIN, ROWS), F32),
            vmem((HEADS, 1, ROWS), F32),
            vmem((HEADS, 1, ROWS), F32),
            vmem((HEADS, 1, ROWS), F32),
            vmem((HEADS, 1, ROWS), F32),
            vmem((HEADS, WIN, ROWS), BF16),
            vmem((HEADS, WIN, ROWS), BF16),
            vmem((HEADS, NLAND * BLK, ROWS), BF16),
            vmem((6 * ROWS, 256), F32),
            vmem((4, NLAND + 1, BLK, 256), F32),
            vmem((2, 4, ROWS, 128), BF16),
            vmem((2, ROWS, 256), BF16),
            vmem((2, ROWS, 256), BF16),
            vmem((2, 4, ROWS, 128), BF16),
            vmem(quad_blocks, F32),
            vmem((depth,) + quad_blocks, BF16),
            vmem((depth,) + quad_blocks, BF16),
            vmem((4,) + quad_blocks, BF16),
            vmem(quad_blocks, F32),
            vmem((2, 4, BLK, 128), BF16),
            DMA((4,)),
            DMA((1,)),
            DMA((6,)),
            DMA((4,)),
            DMA((4,)),
            DMA((4,)),
            DMA((4,)),
            DMA((4,)),
            DMA((4,)),
            DMA((4,)),
            DMA((4,)),
            DMA((depth, 2)),
            DMA((depth, 2)),
            DMA((2, 2)),
            DMA((depth, 2)),
            DMA((2,)),
            DMA((2,)),
            DMA((2, 4)),
            DMA((2, 4)),
            DMA((2,)),
            DMA((2,)),
            DMA((2, 4)),
            DMA((2, 4)),
            DMA((depth,)),
            DMA((depth,)),
            DMA((4,)),
            DMA((4,)),
            DMA((2, 4)),
            DMA((2, 4)),
        ],
        compiler_params=pltpu.CompilerParams(
            collective_id=0, has_side_effects=True, vmem_limit_bytes=VMEM_LIMIT
        ),
    )(
        landmark_cols,
        landmark_rows,
        valid_counts.T,
        queries,
        keys.reshape(block_rows),
        values.reshape(block_rows),
        out_grad,
    )
    return tuple(
        pl.pallas_call(
            emit_kernel,
            out_shape=[shape(flat, BF16)] * 4,
            in_specs=[SM] + [VM] * 6,
            out_specs=[VM] * 4,
        )(landmark_cols, *results)
    )


def solution(mesh):
    n = mesh.shape["prow"]
    tokens = P(("chars", "prow"), None)
    return jax.shard_map(
        functools.partial(per_device, n),
        mesh=mesh,
        in_specs=(tokens, tokens, tokens, tokens, P("chars", None), P("chars"), tokens),
        out_specs=(tokens, tokens, tokens, tokens),
        check_vma=False,
    )
```

```python
import functools

import jax
import jax.numpy as jnp
from jax import lax
from jax.experimental import pallas as pl
from jax.experimental.pallas import tpu as pltpu
from jax.sharding import PartitionSpec as P

HEADS = 8
HD = 64
BLK = 64
NLAND = 4
PC = 4
WIDTH = HEADS * HD
ROWS = PC * BLK
KEYS = 3 * ROWS + NLAND * BLK
F32 = jnp.float32
BF16 = jnp.bfloat16
MESH = pl.DeviceIdType.MESH
masked_score = -1e30
WIN = 3 * ROWS
VMEM_LIMIT = 60 * 1024 * 1024


def dot(a, b):
    return lax.dot_general(a, b, (((1,), (0,)), ((), ())), preferred_element_type=F32)


def remote(src, dst, send, recv, device):
    return pltpu.make_async_remote_copy(
        src_ref=src,
        dst_ref=dst,
        send_sem=send,
        recv_sem=recv,
        device_id={"prow": device},
        device_id_type=MESH,
    )


def position():
    me = lax.axis_index("prow")
    return me, me // 4, me % 4


def neighbours(n):
    me, z, p = position()
    last = n // 4 - 1
    found = [(4 * z + i, p != i) for i in range(4)]
    for step in (1, 2):
        found.append((me + 4 * step, z + step <= last))
        found.append((me - 4 * step, z - step >= 0))
    return found


def greet(n):
    barrier = pltpu.get_barrier_semaphore()
    for device, exists in neighbours(n):

        @pl.when(exists)
        def _():
            pl.semaphore_signal(barrier, inc=1, device_id={"prow": device}, device_id_type=MESH)


def met(n):
    count = 0
    for _, exists in neighbours(n):
        count = count + jnp.where(exists, 1, 0)
    pl.semaphore_wait(pltpu.get_barrier_semaphore(), count)


def fused_kernel(
    n,
    cols_ref,
    rows_ref,
    counts_ref,
    q_in,
    k_in,
    v_in,
    do_in,
    attn_out,
    qgrad_out,
    kgrad_out,
    vgrad_out,
    kland_out,
    vland_out,
    q_ref,
    k_ref,
    v_ref,
    do_ref,
    rows_tx,
    rows_rx,
    rows_quad,
    land_tx,
    k_tx,
    q_tx,
    v_tx,
    d_tx,
    panel_k,
    panel_v,
    kk,
    vv,
    kk_t,
    vv_t,
    qs,
    dd,
    qs_t,
    dd_t,
    lk,
    lv,
    lk_t,
    lv_t,
    bias,
    e_win,
    top_win,
    sum_win,
    scale_win,
    delta_win,
    low_win,
    ds_win,
    prob_land,
    low_land,
    ds_land,
    grads,
    g_land,
    o_tx,
    edge_tx,
    edge_rx,
    g_tx,
    part,
    part_tx,
    relay_rx,
    owner_rx,
    total,
    total_tx,
    load_s,
    local_sem,
    own_s,
    rows_s,
    rows_r,
    land_s,
    land_r,
    in_s,
    in_r,
    panel_up,
    panel_dn,
    panel_far,
    panel_r,
    halo_s,
    halo_r,
    o_s,
    o_r,
    edge_s,
    edge_r,
    g_s,
    g_r,
    relay_s,
    relay_r,
    owner_s,
    owner_r,
    total_s,
    total_r,
):
    me, z, p = position()
    depth = n // 4
    last = depth - 1
    quad = range(4)
    own_col = cols_ref[me]
    greet(n)
    loads = [
        pltpu.make_async_copy(source, place, load_s.at[at])
        for at, (source, place) in enumerate(
            ((k_in, k_ref), (v_in, v_ref), (q_in, q_ref), (do_in, do_ref))
        )
    ]
    for copy in loads:
        copy.start()

    def span(i):
        return slice(i * ROWS, (i + 1) * ROWS)

    def dyn_span(i):
        return pl.ds(pl.multiple_of(i * ROWS, ROWS), ROWS)

    def cols(i):
        return slice(i * 128, (i + 1) * 128)

    loads[0].wait()
    loads[1].wait()
    k_own = k_ref[own_col]
    v_own = v_ref[own_col]
    lane = lax.broadcasted_iota(jnp.int32, (8, 128), 1)
    ints = jnp.zeros((8, 128), jnp.int32)
    for j in range(NLAND):
        ints = jnp.where(lane == j, rows_ref[0, j], ints)
    rows_tx[...] = ints
    rows_rx[p] = ints
    k_rows = k_ref[...].reshape(ROWS, WIDTH)
    v_rows = v_ref[...].reshape(ROWS, WIDTH)
    for i in quad:
        land_tx[0, i] = k_own[:, cols(i)]
        land_tx[1, i] = v_own[:, cols(i)]
        k_tx[i] = k_rows[:, cols(i)]
        v_tx[i] = v_rows[:, cols(i)]

    @pl.when(z == 0)
    def _():
        for rows in (kk, vv):
            rows[span(0)] = jnp.zeros((ROWS, 128), BF16)

    @pl.when(z == last)
    def _():
        for rows in (kk, vv):
            rows[span(5)] = jnp.zeros((ROWS, 128), BF16)

    met(n)

    def rows_to(i):
        return remote(rows_tx, rows_rx.at[p], rows_s.at[i], rows_r.at[p], 4 * z + i)

    def rows_from(i):
        return remote(rows_tx, rows_rx.at[i], rows_s.at[i], rows_r.at[i], 4 * z + i)

    panels = (panel_k, panel_v)

    def land_to(f, i):
        return remote(
            land_tx.at[f, i], panels[f].at[me], land_s.at[f, i], land_r.at[f, p], 4 * z + i
        )

    def land_from(f, i):
        return remote(
            land_tx.at[f, i], panels[f].at[4 * z + i], land_s.at[f, i], land_r.at[f, i], 4 * z + i
        )

    quad_parts = ((k_tx, kk, 1), (q_tx, qs, 0), (v_tx, vv, 1), (d_tx, dd, 0))

    def rows_part_to(f, i):
        source, place, base = quad_parts[f]
        return remote(
            source.at[i], place.at[dyn_span(base + p)], in_s.at[f, i], in_r.at[f, p], 4 * z + i
        )

    def rows_part_from(f, i):
        source, place, base = quad_parts[f]
        return remote(
            source.at[i], place.at[span(base + i)], in_s.at[f, i], in_r.at[f, i], 4 * z + i
        )

    def own_part(f):
        source, place, base = quad_parts[f]
        place[dyn_span(base + p)] = source[p]

    def send_part(f):
        others(lambda i: rows_part_to(f, i).start())

    def part_done(f):
        others(lambda i: rows_part_from(f, i).wait_recv())

    def others(act):
        for i in quad:
            pl.when(p != i)(lambda: act(i))

    def panel_to(f, zz, h, step):
        place = panels[f].at[pl.ds(4 * zz + 2 * h, 2)]
        if step == 1:
            send = panel_up.at[f, zz, h]
        elif step == -1:
            send = panel_dn.at[f, zz, h]
        else:
            send = panel_far.at[f, 0 if step > 0 else 1, h]
        return remote(place, place, send, panel_r.at[f, zz, h], me + 4 * step)

    def panel_own(f, h, act, steps=(2, -2, 1, -1)):
        for step in steps:
            exists = z + step <= last if step > 0 else z + step >= 0
            pl.when(exists)(lambda: act(panel_to(f, z, h, step)))

    def each_side(s, act):
        pl.when(z - s >= 0)(lambda: act(z - s, 1, z < last))
        pl.when(z + s <= last)(lambda: act(z + s, -1, z > 0))

    def panel_relay(f, s, h):
        def step(zz, way, more):
            panel_to(f, zz, h, way).wait_recv()
            pl.when(more)(lambda: panel_to(f, zz, h, way).start())

        each_side(s, step)

    def panel_wait(f, s):
        for h in range(2):
            each_side(s, lambda zz, way, more: panel_to(f, zz, h, way).wait_recv())

    def halo_up(f):
        rows = (kk, vv)[f]
        return remote(
            rows.at[span(4)], rows.at[span(0)], halo_s.at[f, 0], halo_r.at[f, 0], me + 4
        )

    def halo_dn(f):
        rows = (kk, vv)[f]
        return remote(
            rows.at[span(1)], rows.at[span(5)], halo_s.at[f, 1], halo_r.at[f, 1], me - 4
        )

    def send_halo(f):
        pl.when(z < last)(lambda: halo_up(f).start())
        pl.when(z > 0)(lambda: halo_dn(f).start())

    def halo_done(f):
        pl.when(z > 0)(lambda: halo_up(f).wait_recv())
        pl.when(z < last)(lambda: halo_dn(f).wait_recv())

    pos = lax.broadcasted_iota(jnp.int32, (BLK, ROWS), 0)
    qcol = lax.broadcasted_iota(jnp.int32, (BLK, ROWS), 1) // BLK

    def window_bias(i):
        for a in range(3):
            row = 4 * z + i + a - 1
            inside = jnp.logical_and(row >= 0, row < n)
            safe = jnp.clip(row, 0, n - 1)
            for b in range(PC):
                count = jnp.where(inside, counts_ref[b, safe], 0)
                ok = (pos < count) & (qcol >= b - 1) & (qcol <= b + 1)
                base = a * ROWS + b * BLK
                bias[i, base : base + BLK] = jnp.where(ok, 0.0, masked_score)

    def set_queries():
        loads[2].wait()
        for i in quad:
            q_tx[i] = q_ref[:, cols(i)] * 0.125

    def set_grads_in():
        loads[3].wait()
        tpos = lax.broadcasted_iota(jnp.int32, (BLK, WIDTH), 0)
        for b in range(PC):
            at = slice(b * BLK, (b + 1) * BLK)
            part_d = do_ref[at].astype(F32)
            part_d = jnp.where(tpos < counts_ref[b, me], part_d, 0.0).astype(BF16)
            for i in quad:
                d_tx[i, at] = part_d[:, cols(i)]

    def turn(rows, rows_t, a):
        rows_t[:, span(a)] = rows[span(a)].T

    def take_rows():
        others(lambda i: rows_from(i).wait_recv())
        copy = pltpu.make_async_copy(rows_rx, rows_quad, local_sem.at[0])
        copy.start()
        copy.wait()

    def take_land_keys(i):
        for j in range(NLAND):
            row = rows_quad[i, 0, j]
            count = counts_ref[cols_ref[row], row]
            base = WIN + j * BLK
            bias[i, base : base + BLK] = jnp.where(pos < count, 0.0, masked_score)
            lk[i, j * BLK : (j + 1) * BLK] = panel_k[row]

    def take_land_values(i):
        for j in range(NLAND):
            lv[i, j * BLK : (j + 1) * BLK] = panel_v[rows_quad[i, 0, j]]
        lv_t[i] = lv[i].T

    zero = jnp.zeros((HD, ROWS), BF16)

    def padded(rows_t, h):
        return jnp.concatenate([rows_t, zero] if h == 0 else [zero, rows_t], axis=0)

    def window_scores(i):
        k2 = kk[i * ROWS : i * ROWS + WIN]
        for h in range(2):
            head = 2 * i + h
            s = dot(k2, padded(qs_t[h * HD : (h + 1) * HD, span(i)], h)) + bias[i, 0:WIN]
            top = jnp.max(s, axis=0, keepdims=True)
            e = jnp.exp(s - top)
            e_win[head] = e
            top_win[head] = top
            sum_win[head] = jnp.sum(e, axis=0, keepdims=True)

    left = lax.broadcasted_iota(jnp.int32, (ROWS, 128), 1) < HD

    def halved(block, h):
        keep = left if h == 0 else jnp.logical_not(left)
        return jnp.where(keep, block.astype(F32), 0.0).astype(BF16)

    lanes = lax.broadcasted_iota(jnp.int32, (1, ROWS), 1)

    def head_rows(h):
        return slice(h * HD, (h + 1) * HD)

    def land_probs(i):
        q2 = lk[i]
        for h in range(2):
            head = 2 * i + h
            s = dot(q2, padded(qs_t[head_rows(h), span(i)], h)) + bias[i, WIN:KEYS]
            top_w = top_win[head]
            top = jnp.maximum(jnp.max(s, axis=0, keepdims=True), top_w)
            e = jnp.exp(s - top)
            scale_w = jnp.exp(top_w - top)
            inv_total = 1.0 / (jnp.sum(e, axis=0, keepdims=True) + sum_win[head] * scale_w)
            prob_l = e * inv_total
            prob_land[head] = prob_l
            low_land[head] = prob_l.astype(BF16)
            scale_win[head] = scale_w * inv_total

    def store_land(f, i, rows):
        for j in range(NLAND):
            g_land[f, i, j] = rows[j * BLK : (j + 1) * BLK]

    def land_value_grad(i):
        do2 = dd[span(i)]
        store_land(
            1,
            i,
            dot(low_land[2 * i], halved(do2, 0)) + dot(low_land[2 * i + 1], halved(do2, 1)),
        )

    def land_key_grad(i):
        win = slice(i * ROWS, i * ROWS + WIN)
        q2 = qs[span(i)]
        v2 = lv[i]
        dk2 = 0.0
        mixes = []
        for h in range(2):
            head = 2 * i + h
            rows = head_rows(h)
            low_w = (e_win[head] * scale_win[head]).astype(BF16)
            low_win[head] = low_w
            mixed = dot(vv_t[rows, win], low_w) + dot(lv_t[i, rows, :], low_land[head])
            mixes.append(mixed)
            dot_t = dd_t[rows, span(i)]
            delta = jnp.sum(dot_t.astype(F32) * mixed, axis=0, keepdims=True)
            delta_win[head] = delta
            ds_l = (prob_land[head] * (dot(v2, padded(dot_t, h)) - delta)).astype(BF16)
            ds_land[head] = ds_l
            dk2 = dk2 + dot(ds_l, halved(q2, h))
        store_land(0, i, dk2)
        valid = jnp.zeros((1, ROWS), jnp.bool_)
        for b in range(PC):
            valid = valid | ((lanes >= b * BLK) & (lanes < b * BLK + counts_ref[b, 4 * z + i]))
        mixed = jnp.where(valid, jnp.concatenate(mixes, axis=0), 0.0)
        send_output(0, i, mixed.T.astype(BF16))

    def window_scores_grad(i):
        win = slice(i * ROWS, i * ROWS + WIN)
        v2w = vv[win]
        dqs = []
        lk_t[i] = lk[i].T
        for h in range(2):
            head = 2 * i + h
            rows = head_rows(h)
            prob_w = e_win[head] * scale_win[head]
            dot_w = padded(dd_t[rows, span(i)], h)
            ds_w = (prob_w * (dot(v2w, dot_w) - delta_win[head])).astype(BF16)
            ds_win[head] = ds_w
            dqs.append((dot(kk_t[rows, win], ds_w) + dot(lk_t[i, rows, :], ds_land[head])) * 0.125)
        send_output(1, i, jnp.concatenate(dqs, axis=0).T.astype(BF16))

    my_cols = pl.ds(pl.multiple_of(p * 128, 128), 128)

    def piece_to(at, src, out, sends, recvs, i):
        return remote(src, out.at[:, my_cols], sends.at[at, i], recvs.at[at, p], 4 * z + i)

    def piece_from(at, src, out, sends, recvs, i):
        return remote(src, out.at[:, cols(i)], sends.at[at, i], recvs.at[at, i], 4 * z + i)

    def piece_own(at, src, out, i):
        return pltpu.make_async_copy(src, out.at[:, cols(i)], own_s.at[at])

    def deliver(at, src, out, sends, recvs, i):
        pl.when(p != i)(lambda: piece_to(at % 2, src, out, sends, recvs, i).start())
        pl.when(p == i)(lambda: piece_own(at, src, out, i).start())

    def delivered(at, srcs, out, sends, recvs):
        for i in quad:
            src = srcs.at[at % 2, i]

            @pl.when(p != i)
            def _():
                piece_from(at % 2, src, out, sends, recvs, i).wait_recv()

            pl.when(p == i)(lambda: piece_own(at, src, out, i).wait())

    def sent(at, srcs, out, sends, recvs):
        for i in quad:
            src = srcs.at[at % 2, i]
            pl.when(p != i)(
                lambda: piece_to(at % 2, src, out, sends, recvs, i).wait_send()
            )

    out_plan = (
        (0, o_tx, attn_out, o_s, o_r),
        (1, o_tx, qgrad_out, o_s, o_r),
        (2, g_tx, kgrad_out, g_s, g_r),
        (3, g_tx, vgrad_out, g_s, g_r),
        (4, total_tx, kland_out, total_s, total_r),
        (5, total_tx, vland_out, total_s, total_r),
    )

    def send_piece(at, i):
        _, srcs, out, sends, recvs = out_plan[at]
        deliver(at, srcs.at[at % 2, i], out, sends, recvs, i)

    def send_output(f, i, rows):
        o_tx[f, i] = rows
        send_piece(f, i)

    touched = set()

    def edge_up():
        return remote(edge_tx.at[0], edge_rx.at[0], edge_s.at[0], edge_r.at[0], me + 4)

    def edge_dn():
        return remote(edge_tx.at[1], edge_rx.at[1], edge_s.at[1], edge_r.at[1], me - 4)

    def window_grads(i):
        q2, do2 = qs[span(i)], dd[span(i)]
        dk2 = dot(ds_win[2 * i], halved(q2, 0)) + dot(ds_win[2 * i + 1], halved(q2, 1))
        dv2 = dot(low_win[2 * i], halved(do2, 0)) + dot(low_win[2 * i + 1], halved(do2, 1))
        for term, at in ((dk2, slice(0, 128)), (dv2, slice(128, 256))):
            for a in range(3):
                piece = term[span(a)]
                if i + a == 0:
                    edge_tx[1, :, at] = piece.astype(BF16)
                elif i + a == 5:
                    edge_tx[0, :, at] = piece.astype(BF16)
                elif (i + a, at.start) in touched:
                    grads[span(i + a), at] = grads[span(i + a), at] + piece
                else:
                    touched.add((i + a, at.start))
                    grads[span(i + a), at] = piece
        if i == 0:
            pl.when(z > 0)(lambda: edge_dn().start())
        if i == 3:
            pl.when(z < last)(lambda: edge_up().start())

    def send_grads(i):
        if i == 0:

            @pl.when(z > 0)
            def _():
                edge_up().wait_recv()
                grads[span(1)] = grads[span(1)] + edge_rx[0].astype(F32)

        if i == 3:

            @pl.when(z < last)
            def _():
                edge_dn().wait_recv()
                grads[span(4)] = grads[span(4)] + edge_rx[1].astype(F32)

        both = grads[span(1 + i)].astype(BF16)
        for f in range(2):
            g_tx[f, i] = both[:, cols(f)]
            send_piece(2 + f, i)

    def slot_of(i, row):
        found = NLAND
        for j in range(NLAND):
            found = jnp.where(rows_quad[i, 0, j] == row, j, found)
        return found

    def gathered(f, row):
        return sum(g_land[f, i, slot_of(i, row)] for i in quad)

    def relay(f, zz, way):
        return remote(
            part_tx.at[f, zz], relay_rx.at[f, zz], relay_s.at[f, zz], relay_r.at[f, zz], me - 4 * way
        )

    def to_owner(f, zz, way, s):
        code = (0 if way > 0 else 2) + s - 1
        return remote(
            part_tx.at[f, zz],
            owner_rx.at[f, code],
            owner_s.at[f, code],
            owner_r.at[f, code],
            me - 4 * way * s,
        )

    def reduce_step(f, s):
        def step(zz, way, more):
            for t in quad:
                part[t] = gathered(f, 4 * zz + t)
            if s >= 2:

                @pl.when(more)
                def _():
                    relay(f, zz, way).wait_recv()
                    part[...] = part[...] + relay_rx[f, zz].astype(F32)

            part_tx[f, zz] = part[...].astype(BF16)
            if s >= 3:
                relay(f, zz, way).start()
            else:
                to_owner(f, zz, way, s).start()

        each_side(s, step)

    def reduce_own(f):
        for t in quad:
            total[f, t] = gathered(f, 4 * z + t)

    def reduce_finish(f):
        for s in (1, 2):
            for way in (1, -1):
                exists = z + s <= last if way > 0 else z - s >= 0

                @pl.when(exists)
                def _():
                    to_owner(f, z, way, s).wait_recv()
                    code = (0 if way > 0 else 2) + s - 1
                    total[f] = total[f] + owner_rx[f, code].astype(F32)

        for t in quad:
            total_tx[f, t] = total[f, t].astype(BF16)
            send_piece(4 + f, t)

    def outputs_done():
        for plan in out_plan:
            delivered(*plan)

    def gather_sent():
        others(lambda i: rows_to(i).wait_send())
        for f in range(2):
            others(lambda i: land_to(f, i).wait_send())
            for h in range(2):
                panel_own(f, h, lambda copy: copy.wait_send())
                for s in range(2, last):
                    each_side(
                        s,
                        lambda zz, way, more: pl.when(more)(
                            lambda: panel_to(f, zz, h, way).wait_send()
                        ),
                    )
            pl.when(z < last)(lambda: halo_up(f).wait_send())
            pl.when(z > 0)(lambda: halo_dn(f).wait_send())
        for f in range(4):
            others(lambda i: rows_part_to(f, i).wait_send())

    def reduce_sent():
        pl.when(z < last)(lambda: edge_up().wait_send())
        pl.when(z > 0)(lambda: edge_dn().wait_send())
        for s in range(1, last + 1):

            def step(zz, way, more):
                for f in range(2):
                    (relay(f, zz, way) if s >= 3 else to_owner(f, zz, way, s)).wait_send()

            each_side(s, step)
        for plan in out_plan:
            sent(*plan)

    y = p // 2

    def land_near(f):
        for i in quad:
            pl.when(jnp.logical_and(i // 2 == y, i != p))(lambda: land_from(f, i).wait_recv())

    def land_across(f):
        for i in quad:
            pl.when(i // 2 != y)(lambda: land_from(f, i).wait_recv())

    def start(copy):
        copy.start()

    def relays(f):
        for s in range(2, last):
            panel_relay(f, s, y)
            panel_relay(f, s, 1 - y)

    for f in range(2):
        others(lambda i: land_to(f, i).start())
    send_part(0)
    others(lambda i: rows_to(i).start())
    for f in range(2):
        panels[f][me] = land_tx[f, p]
    land_near(0)
    panel_own(0, y, start)
    set_queries()
    send_part(1)
    send_part(2)
    land_across(0)
    panel_own(0, 1 - y, start)
    set_grads_in()
    send_part(3)
    land_near(1)
    panel_own(1, y, start)
    land_across(1)
    panel_own(1, 1 - y, start)
    for f in range(4):
        own_part(f)
    for i in quad:
        for f in range(2):
            g_land[f, i, NLAND] = jnp.zeros((BLK, 128), F32)
        window_bias(i)
    relays(0)
    part_done(0)
    send_halo(0)
    take_rows()
    for i in quad:
        turn(kk, kk_t, 1 + i)
    part_done(1)
    for i in quad:
        turn(qs, qs_t, i)
    relays(1)
    window_scores(1)
    part_done(2)
    send_halo(1)
    window_scores(2)
    halo_done(0)
    turn(kk, kk_t, 0)
    turn(kk, kk_t, 5)
    window_scores(0)
    window_scores(3)
    for i in quad:
        turn(vv, vv_t, 1 + i)
    for s in sorted({1, last} - {0}):
        panel_wait(0, s)
    for i in quad:
        take_land_keys(i)
        land_probs(i)
    part_done(3)
    for i in quad:
        turn(dd, dd_t, i)
        land_value_grad(i)
    for s in range(last, 2, -1):
        reduce_step(1, s)
    if last > 0:
        reduce_step(1, 1)
    for s in sorted({1, last} - {0}):
        panel_wait(1, s)
    for i in (1, 2):
        take_land_values(i)
        land_key_grad(i)
    halo_done(1)
    turn(vv, vv_t, 0)
    turn(vv, vv_t, 5)
    for i in (0, 3):
        take_land_values(i)
        land_key_grad(i)
    for s in range(last, 2, -1):
        reduce_step(0, s)
    if last > 0:
        reduce_step(0, 1)
    if last > 1:
        reduce_step(1, 2)
    for i in (0, 3):
        window_scores_grad(i)
        window_grads(i)
    if last > 1:
        reduce_step(0, 2)
    for i in (1, 2):
        window_scores_grad(i)
        window_grads(i)
    send_grads(1)
    send_grads(2)
    for f in range(2):
        reduce_own(f)
    send_grads(0)
    send_grads(3)
    gather_sent()
    reduce_finish(1)
    reduce_finish(0)
    reduce_sent()
    outputs_done()


def emit_kernel(cols_ref, attn, qgrad, kgrad, vgrad, kland, vland, *results):
    own_col = cols_ref[lax.axis_index("prow")]
    results[0][...] = attn[...]
    results[1][...] = qgrad[...]
    for source, land, result in ((kgrad, kland, results[2]), (vgrad, vland, results[3])):
        term = land[...].astype(F32)
        for b in range(PC):
            at = slice(b * BLK, (b + 1) * BLK)
            result[at] = (source[at].astype(F32) + jnp.where(own_col == b, term, 0.0)).astype(BF16)


VM = pl.BlockSpec(memory_space=pltpu.VMEM)
SM = pl.BlockSpec(memory_space=pltpu.SMEM)
ANY = pl.BlockSpec(memory_space=pl.ANY)
DMA = pltpu.SemaphoreType.DMA


def shape(dims, dtype):
    return jax.ShapeDtypeStruct(dims, dtype)


def per_device(n, queries, keys, values, out_grad, valid_counts, landmark_cols, landmark_rows):
    depth = n // 4
    flat = (ROWS, WIDTH)
    block_rows = (PC, BLK, WIDTH)
    quad_rows = (4, ROWS, 128)
    quad_blocks = (4, BLK, 128)
    vmem = pltpu.VMEM
    results = pl.pallas_call(
        functools.partial(fused_kernel, n),
        out_shape=[shape(flat, BF16)] * 4 + [shape((BLK, WIDTH), BF16)] * 2,
        in_specs=[SM] * 3 + [ANY] * 4,
        out_specs=[ANY] * 6,
        scratch_shapes=[
            vmem(flat, BF16),
            vmem(block_rows, BF16),
            vmem(block_rows, BF16),
            vmem(flat, BF16),
            vmem((8, 128), jnp.int32),
            vmem((4, 8, 128), jnp.int32),
            pltpu.SMEM((4, 8, 128), jnp.int32),
            vmem((2,) + quad_blocks, BF16),
            vmem(quad_rows, BF16),
            vmem(quad_rows, BF16),
            vmem(quad_rows, BF16),
            vmem(quad_rows, BF16),
            vmem((n, BLK, 128), BF16),
            vmem((n, BLK, 128), BF16),
            vmem((6 * ROWS, 128), BF16),
            vmem((6 * ROWS, 128), BF16),
            vmem((128, 6 * ROWS), BF16),
            vmem((128, 6 * ROWS), BF16),
            vmem((4 * ROWS, 128), BF16),
            vmem((4 * ROWS, 128), BF16),
            vmem((128, 4 * ROWS), BF16),
            vmem((128, 4 * ROWS), BF16),
            vmem((4, NLAND * BLK, 128), BF16),
            vmem((4, NLAND * BLK, 128), BF16),
            vmem((4, 128, NLAND * BLK), BF16),
            vmem((4, 128, NLAND * BLK), BF16),
            vmem((4, KEYS, ROWS), F32),
            vmem((HEADS, WIN, ROWS), F32),
            vmem((HEADS, 1, ROWS), F32),
            vmem((HEADS, 1, ROWS), F32),
            vmem((HEADS, 1, ROWS), F32),
            vmem((HEADS, 1, ROWS), F32),
            vmem((HEADS, WIN, ROWS), BF16),
            vmem((HEADS, WIN, ROWS), BF16),
            vmem((HEADS, NLAND * BLK, ROWS), F32),
            vmem((HEADS, NLAND * BLK, ROWS), BF16),
            vmem((HEADS, NLAND * BLK, ROWS), BF16),
            vmem((6 * ROWS, 256), F32),
            vmem((2, 4, NLAND + 1, BLK, 128), F32),
            vmem((2, 4, ROWS, 128), BF16),
            vmem((2, ROWS, 256), BF16),
            vmem((2, ROWS, 256), BF16),
            vmem((2, 4, ROWS, 128), BF16),
            vmem(quad_blocks, F32),
            vmem((2, depth) + quad_blocks, BF16),
            vmem((2, depth) + quad_blocks, BF16),
            vmem((2, 4) + quad_blocks, BF16),
            vmem((2,) + quad_blocks, F32),
            vmem((2, 4, BLK, 128), BF16),
            DMA((4,)),
            DMA((1,)),
            DMA((6,)),
            DMA((4,)),
            DMA((4,)),
            DMA((2, 4)),
            DMA((2, 4)),
            DMA((4, 4)),
            DMA((4, 4)),
            DMA((2, depth, 2)),
            DMA((2, depth, 2)),
            DMA((2, 2, 2)),
            DMA((2, depth, 2)),
            DMA((2, 2)),
            DMA((2, 2)),
            DMA((2, 4)),
            DMA((2, 4)),
            DMA((2,)),
            DMA((2,)),
            DMA((2, 4)),
            DMA((2, 4)),
            DMA((2, depth)),
            DMA((2, depth)),
            DMA((2, 4)),
            DMA((2, 4)),
            DMA((2, 4)),
            DMA((2, 4)),
        ],
        compiler_params=pltpu.CompilerParams(
            collective_id=0, has_side_effects=True, vmem_limit_bytes=VMEM_LIMIT
        ),
    )(
        landmark_cols,
        landmark_rows,
        valid_counts.T,
        queries,
        keys.reshape(block_rows),
        values.reshape(block_rows),
        out_grad,
    )
    return tuple(
        pl.pallas_call(
            emit_kernel,
            out_shape=[shape(flat, BF16)] * 4,
            in_specs=[SM] + [VM] * 6,
            out_specs=[VM] * 4,
        )(landmark_cols, *results)
    )


def solution(mesh):
    n = mesh.shape["prow"]
    tokens = P(("chars", "prow"), None)
    return jax.shard_map(
        functools.partial(per_device, n),
        mesh=mesh,
        in_specs=(tokens, tokens, tokens, tokens, P("chars", None), P("chars"), tokens),
        out_specs=(tokens, tokens, tokens, tokens),
        check_vma=False,
    )
```
